32 devices in a mesh: mesh: 16 (over z, x, core), band: 2 (over y).
Axes of the slice: x: 2, y: 2, z: 4, core: 2. Of those that a mesh axis runs over, the one named last changes fastest.
Arguments:
- band_block: bfloat16 [320, 4096], P('band', 'mesh'), may hold values from -6 to 6
- band_basis: bfloat16 [4096, 3072], P('mesh', 'band'), may hold values from -0.25 to 0.25
- mass_scale: float32 [4096], P('mesh'), may hold values from 0.7 to 1.5
- cell_matrices: bfloat16 [256, 4096], P('mesh')
- cell_nodes: int32 [256, 64], P('mesh'), may hold values from 0 to 319, as said below
- cell_count: int32 [16], P('mesh'), may hold values from 8 to 16, as said below
- send_index: int32 [16, 4, 16], P('mesh'), may hold values from 0 to 256, as said below
Outputs:
- filtered: bfloat16 [320, 4096], P('band', 'mesh')
- intersection: float32 [3072, 320], P('mesh', 'band')
- hamiltonian: float32 [3072, 320], P('mesh', 'band')
The draws below stay inside these ranges and needn't reach their ends.
Inputs may be any that keep to these rules, and one draw needn't show every extreme that they name: `cell_nodes`: an entry below 256 is an owned node of the cell's partition; an entry 256 + k * 16 + c names ghost c of neighbour slot k, and c is always below the number of nodes that neighbour lists for this partition. In some partition the first cell's first entry is the last ghost slot, 319. send_index[p, k, :] lists, in ghost-slot order, owned nodes of partition p held by the partition (p + off(k)) mod 16; used slots come first and 256 marks an unused slot. Only partitions within 2 index steps (cyclically) share nodes. Some partition lists 16 nodes toward every neighbour and receives 16 from every neighbour. `cell_count`: some partition has all 16 cells live.
All inputs are finite; a program needn't handle non-finite values.
Results may differ from the reference program's by a relative error of at most 0.012.
Values may be sent and summed in bfloat16 or wider, within the bound.
A program may use at most 64 MiB of HBM per device.

```python
import math
import jax
import jax.numpy as jnp
from jax import lax

BANDS = 3072
NPC = 64
REACH = 2
NODES_DEV = 256
CELLS_DEV = 16
SLOTS = 16
PARTS_SIZE = 16
NODES = 4096
BLOCKS = 320


def slot_offsets():
    slot_index = jnp.arange(2 * REACH, dtype=jnp.int32)
    offsets = jnp.where(slot_index < REACH, slot_index + 1, REACH - 1 - slot_index).astype(jnp.int32)
    partners = ((slot_index + REACH) % (2 * REACH)).astype(jnp.int32)
    return (offsets, partners)


def slot_counts(key):
    base = jax.random.fold_in(key, 71)
    first_key, second_key = jax.random.split(base)
    counts = jax.random.randint(first_key, (PARTS_SIZE, 2 * REACH), SLOTS // 2, SLOTS + 1)
    chosen = jax.random.randint(second_key, (), 0, PARTS_SIZE)
    offsets, partners = slot_offsets()
    owners = jnp.arange(PARTS_SIZE, dtype=jnp.int32)[:, None]
    target = (owners + offsets[None, :]) % PARTS_SIZE
    full = jnp.logical_or(target == chosen, owners == chosen)
    return (jnp.where(full, SLOTS, counts).astype(jnp.int32), chosen)


def draw_send_index(key, part):
    counts, chosen = slot_counts(key)
    picks = jax.random.randint(jax.random.fold_in(key, 5), (PARTS_SIZE, 2 * REACH, SLOTS), 0, NODES_DEV)
    position = jnp.arange(SLOTS, dtype=jnp.int32)[None, None, :]
    return jnp.where(position < counts[:, :, None], picks, NODES_DEV).astype(jnp.int32)


def draw_cell_nodes(key, part):
    counts, chosen = slot_counts(key)
    offsets, partners = slot_offsets()
    owners = jnp.arange(PARTS_SIZE, dtype=jnp.int32)[:, None]
    incoming = counts[(owners + offsets[None, :]) % PARTS_SIZE, partners[None, :]]
    keys = jax.random.split(jax.random.fold_in(key, 9), 4)
    shape = (PARTS_SIZE, CELLS_DEV, NPC)
    is_ghost = jax.random.randint(keys[0], shape, 0, 5) == 0
    neighbour = jax.random.randint(keys[1], shape, 0, 2 * REACH)
    raw_pos = jax.random.randint(keys[2], shape, 0, 1 << 20)
    owned = jax.random.randint(keys[3], shape, 0, NODES_DEV)
    part_ids = jnp.arange(PARTS_SIZE, dtype=jnp.int32)[:, None, None]
    limit = incoming[part_ids, neighbour]
    ghost_value = NODES_DEV + neighbour * SLOTS + raw_pos % limit
    nodes = jnp.where(is_ghost, ghost_value, owned).astype(jnp.int32)
    nodes = nodes.at[chosen, 0, 0].set(NODES_DEV + 2 * REACH * SLOTS - 1)
    nodes = nodes.at[chosen, 0, 1].set(0)
    return nodes.reshape(PARTS_SIZE * CELLS_DEV, NPC)


def draw_cell_count(key, part):
    first_key, second_key = jax.random.split(jax.random.fold_in(key, 13))
    counts = jax.random.randint(first_key, (PARTS_SIZE,), CELLS_DEV // 2, CELLS_DEV + 1)
    chosen = jax.random.randint(second_key, (), 0, PARTS_SIZE)
    counts = counts.at[chosen].set(CELLS_DEV)
    counts = counts.at[(chosen + 1) % PARTS_SIZE].set(CELLS_DEV // 2)
    return counts.astype(jnp.int32)


def draw_cell_matrices(key, part):
    shape = (PARTS_SIZE * CELLS_DEV, NPC, NPC)
    entries = jax.random.normal(key, shape, jnp.float32)
    symmetric = (entries + jnp.swapaxes(entries, 1, 2)) * (0.5 / math.sqrt(2.0 * NPC))
    return symmetric.reshape(PARTS_SIZE * CELLS_DEV, NPC * NPC).astype(jnp.bfloat16)


def strengthened(values, key, source, target, parts, factor):
    owner, partner = [(jnp.arange(values.shape[axis_at]) // (values.shape[axis_at] // parts)).reshape([-1 if axis == axis_at else 1 for axis in range(values.ndim)]) for axis_at in (source, target)]
    chosen = jax.random.permutation(key, parts)[partner]
    strong = (owner == chosen) | (owner == (partner + parts // 2) % parts)
    return jnp.where(strong, factor * values, values)


def block_scale(own_key, extent, cuts, smallest, high):
    def one(dim, shards_of):
        steps = jax.random.uniform(jax.random.fold_in(jax.random.fold_in(own_key, 6), dim), (shards_of,), jnp.float32, smallest / len(cuts), high / len(cuts))
        return jnp.repeat(jnp.exp(steps), extent[dim] // shards_of).reshape((-1,) + (1,) * (len(extent) - dim - 1))

    gain = one(*cuts[0])
    for cut in cuts[1:]:
        gain = gain * one(*cut)
    return gain


def gaussian(stream_key, shape, scale, most, cuts=(), kind=jnp.bfloat16):
    level = block_scale(stream_key, shape, cuts, -0.22, 0.18) if cuts else 1.0
    result = jax.random.normal(stream_key, shape, jnp.float32) * scale * level
    return jnp.minimum(jnp.maximum(result, -most), most).astype(kind)


def noise_with(stream_key, extent, scale, most, shards, heavy, held_as=jnp.bfloat16):
    array = scale * jax.random.normal(stream_key, extent, jnp.float32)
    if shards:
        array = array * block_scale(stream_key, extent, shards, -0.22, 0.18)
    return jnp.clip(strengthened(array, jax.random.fold_in(stream_key, 3), *heavy), -most, most).astype(held_as)


def setup_inputs(seed: int = 0) -> dict:
    splits = jax.random.split(jax.random.key(seed), 8)
    band_block = gaussian(splits[0], (BLOCKS, NODES), 1.0, 6.0, ((0, 2), (1, 16)))
    band_basis = noise_with(splits[1], (NODES, BANDS), (NODES // 4) ** -0.5, 0.25, ((0, 16), (1, 2)), (0, 1, 16, 2.0))
    mass_scale = jnp.clip(jnp.exp(math.log(1.5) - 0.7621401 * jax.random.uniform(splits[2], (NODES,), jnp.float32) ** block_scale(splits[2], (NODES,), ((0, 16),), -0.2, 0.2)), 0.7, 1.5)
    cell_matrices = draw_cell_matrices(jax.random.fold_in(splits[7], 71), 0)
    cell_nodes = draw_cell_nodes(jax.random.fold_in(splits[7], 71), 0)
    cell_count = draw_cell_count(jax.random.fold_in(splits[7], 71), 0)
    send_index = draw_send_index(jax.random.fold_in(splits[7], 71), 0)
    return {"band_block": band_block, "band_basis": band_basis, "mass_scale": mass_scale, "cell_matrices": cell_matrices, "cell_nodes": cell_nodes, "cell_count": cell_count, "send_index": send_index}


filter_centre = 1.5
filter_half = 2.5
first_sigma = -0.625


def sigma_values():
    values = [first_sigma]
    for _ in range(2):
        values.append(1.0 / (2.0 / first_sigma - values[-1]))
    return values


def global_node_ids(cell_nodes, send_index):
    width = 2 * REACH
    slot_index = jnp.arange(width, dtype=jnp.int32)
    offsets = jnp.where(slot_index < REACH, slot_index + 1, REACH - 1 - slot_index).astype(jnp.int32)
    partners = ((slot_index + REACH) % width).astype(jnp.int32)
    local_ids = cell_nodes.reshape(PARTS_SIZE, CELLS_DEV, NPC)
    owner_part = jnp.arange(PARTS_SIZE, dtype=jnp.int32)[:, None, None]
    ghost_pos = jnp.maximum(local_ids - NODES_DEV, 0)
    neighbour = jnp.minimum(ghost_pos // SLOTS, width - 1)
    position = ghost_pos % SLOTS
    source = (owner_part + offsets[neighbour]) % PARTS_SIZE
    remote = send_index[source, partners[neighbour], position]
    return jnp.where(local_ids < NODES_DEV, owner_part * NODES_DEV + local_ids, source * NODES_DEV + remote).astype(jnp.int32)


def reference(band_block, band_basis, mass_scale, cell_matrices, cell_nodes, cell_count, send_index):
    node_ids = global_node_ids(cell_nodes, send_index)
    live_mask = (jnp.arange(CELLS_DEV, dtype=jnp.int32)[None, :] < cell_count[:, None]).astype(jnp.float32)
    matrices = cell_matrices.reshape(PARTS_SIZE, CELLS_DEV, NPC, NPC)
    columns = band_block.shape[0]

    def operate(field):
        scaled = (mass_scale[None, :] * field.astype(jnp.float32)).astype(jnp.bfloat16)

        def one_part(summed, inputs):
            part_ids, part_mats, part_live = inputs
            gathered = scaled[:, part_ids].astype(jnp.float32)
            products = jnp.einsum("cij,bcj->bci", part_mats.astype(jnp.float32), gathered)
            products = products * part_live[None, :, None]
            summed = summed.at[:, part_ids.reshape(-1)].add(products.reshape(columns, -1))
            return summed, None

        summed, _ = lax.scan(one_part, jnp.zeros((columns, NODES), jnp.float32), (node_ids, matrices, live_mask))
        return mass_scale[None, :] * summed

    sigmas = sigma_values()
    previous = band_block
    applied = operate(band_block)
    current = ((applied - filter_centre * band_block.astype(jnp.float32)) * (sigmas[0] / filter_half)).astype(jnp.bfloat16)
    for step in range(1, 3):
        applied = operate(current)
        scale_now = 2.0 * sigmas[step] / filter_half
        mixing = sigmas[step - 1] * sigmas[step]
        update = (applied - filter_centre * current.astype(jnp.float32)) * scale_now - mixing * previous.astype(jnp.float32)
        previous = current
        current = update.astype(jnp.bfloat16)
    filtered = current
    image = operate(filtered).astype(jnp.bfloat16)
    dims = (((0,), (1,)), ((), ()))
    intersection = lax.dot_general(band_basis, filtered, dims, preferred_element_type=jnp.float32)
    hamiltonian = lax.dot_general(band_basis, image, dims, preferred_element_type=jnp.float32)
    return filtered, intersection, hamiltonian
```

```python
import functools
import jax
import jax.numpy as jnp
from jax import lax
from jax.experimental import pallas as pl
from jax.experimental.pallas import tpu as pltpu
from jax.sharding import PartitionSpec as P

filter_centre = 1.5
filter_half = 2.5
first_sigma = -0.625
MESH = pl.DeviceIdType.MESH
bf16 = jnp.bfloat16
f32 = jnp.float32


def sigma_values():
    values = [first_sigma]
    for _ in range(2):
        values.append(1.0 / (2.0 / first_sigma - values[-1]))
    return values


def neighbour_offset(neighbour, reach):
    if neighbour < reach:
        return neighbour + 1
    return reach - 1 - neighbour


def dot(a, b):
    return jnp.dot(a, b, preferred_element_type=f32)


def kernel(
    n, nb, width, x_ref, basis_ref, mass_ref, mats_ref, ncol_ref, nrow_ref, scol_ref, srow_ref,
    f_ref, inter_ref, ham_ref,
    full, stiff, coupled, fields, out_x, ghost, out_y, back, tile, got,
    halo_send, halo_recv, basis_send, basis_recv, local_sem, tile_send, tile_recv,
):
    me = lax.axis_index("mesh")
    mine = lax.axis_index("band")
    columns, owned = x_ref.shape
    slots = scol_ref.shape[0] // width
    reach = width // 2
    cols = basis_ref.shape[0]
    rows = full.shape[0] // n
    total = owned + width * slots

    barrier = pltpu.get_barrier_semaphore()

    def greet(d, carry):
        pl.semaphore_signal(
            barrier, inc=1, device_id=(lax.rem(me + d, n), mine), device_id_type=MESH
        )
        return carry

    lax.fori_loop(1, n, greet, 0)
    for d in range(1, nb):
        pl.semaphore_signal(
            barrier, inc=1, device_id=(me, lax.rem(mine + d, nb)), device_id_type=MESH
        )

    my_rows = pl.ds(pl.multiple_of(mine * cols, 16), cols)
    local = pltpu.make_async_copy(basis_ref, full.at[my_rows], local_sem)
    local.start()

    mass = mass_ref[...]
    send_hot = jnp.where(
        lax.broadcasted_iota(jnp.int32, (width * slots, owned), 1) == scol_ref[...], 1.0, 0.0
    ).astype(bf16)
    send_hot_t = jnp.where(
        lax.broadcasted_iota(jnp.int32, (owned, width * slots), 0) == srow_ref[...], 1.0, 0.0
    ).astype(bf16)

    pl.semaphore_wait(barrier, n - 1 + nb - 1)

    def halo(source, target, index):
        copies = []
        for k in range(width):
            partner = (k + reach) % width
            to = lax.rem(me + neighbour_offset(k, reach) + n, n)
            copies.append(
                pltpu.make_async_remote_copy(
                    src_ref=source.at[pl.ds(k * slots, slots)],
                    dst_ref=target.at[pl.ds(partner * slots, slots)],
                    send_sem=halo_send.at[index, k],
                    recv_sem=halo_recv.at[index, partner],
                    device_id=(to, mine),
                    device_id_type=MESH,
                )
            )
        return copies

    def assemble():
        corners = mats_ref.shape[1]
        for c in range(mats_ref.shape[0] // corners):
            part = pl.ds(c * corners, corners)
            hot = jnp.where(
                lax.broadcasted_iota(jnp.int32, (corners, total), 1) == ncol_ref[part, :], 1.0, 0.0
            ).astype(bf16)
            coupled[part, :] = dot(mats_ref[part, :], hot).astype(bf16)
        hot_t = jnp.where(
            lax.broadcasted_iota(jnp.int32, (total, mats_ref.shape[0]), 0) == nrow_ref[...], 1.0, 0.0
        ).astype(bf16)
        stiff[...] = dot(hot_t, coupled[...]).astype(bf16)

    started = []

    def operate(step, field):
        scaled = (mass * field.astype(f32)).astype(bf16)
        out_x[step] = dot(send_hot, scaled).astype(bf16)
        copies = halo(out_x.at[step], ghost.at[step], 2 * step)
        for copy in copies:
            copy.start()
        started.extend(copies)
        if step == 0:
            for d in range(1, nb):
                copy = pltpu.make_async_remote_copy(
                    src_ref=basis_ref,
                    dst_ref=full.at[my_rows],
                    send_sem=basis_send.at[d],
                    recv_sem=basis_recv.at[d],
                    device_id=(me, lax.rem(mine + d, nb)),
                    device_id_type=MESH,
                )
                copy.start()
            assemble()
        edge = dot(stiff[owned:, :owned], scaled)
        inner = dot(stiff[:owned, :owned], scaled)
        for copy in copies:
            copy.wait_recv()
        ghosts = ghost[step]
        out_y[step] = (edge + dot(stiff[owned:, owned:], ghosts)).astype(bf16)
        copies = halo(out_y.at[step], back.at[step], 2 * step + 1)
        for copy in copies:
            copy.start()
        started.extend(copies)
        inner = inner + dot(stiff[:owned, owned:], ghosts)
        for copy in copies:
            copy.wait_recv()
        return mass * (inner + dot(send_hot_t, back[step]))

    sigmas = sigma_values()
    previous = x_ref[...].astype(f32).T.astype(bf16)
    applied = operate(0, previous)
    current = (
        (applied - filter_centre * previous.astype(f32)) * (sigmas[0] / filter_half)
    ).astype(bf16)
    for step in range(1, 3):
        applied = operate(step, current)
        scale_now = 2.0 * sigmas[step] / filter_half
        mixing = sigmas[step - 1] * sigmas[step]
        update = (applied - filter_centre * current.astype(f32)) * scale_now - mixing * previous.astype(f32)
        previous = current
        current = update.astype(bf16)
    image = operate(3, current)
    f_ref[...] = current.astype(f32).T.astype(bf16)
    fields[...] = jnp.concatenate([current.astype(f32), image], axis=1).astype(bf16)

    local.wait()
    for d in range(1, nb):
        source = lax.rem(mine + nb - d, nb)
        its_rows = pl.ds(pl.multiple_of(source * cols, 16), cols)
        copy = pltpu.make_async_remote_copy(
            src_ref=basis_ref,
            dst_ref=full.at[its_rows],
            send_sem=basis_send.at[d],
            recv_sem=basis_recv.at[d],
            device_id=(me, lax.rem(mine + d, nb)),
            device_id_type=MESH,
        )
        copy.wait_send()
        copy.wait_recv()

    def tile_copy(d):
        return pltpu.make_async_remote_copy(
            src_ref=tile.at[d],
            dst_ref=got.at[d],
            send_sem=tile_send.at[d],
            recv_sem=tile_recv.at[d],
            device_id=(lax.rem(me + d, n), mine),
            device_id_type=MESH,
        )

    def product(target):
        return dot(full[pl.ds(pl.multiple_of(target * rows, 16), rows), :], fields[...])

    def emit(d, carry):
        tile[d] = product(lax.rem(me + d, n)).astype(bf16)
        tile_copy(d).start()
        return carry

    lax.fori_loop(1, n, emit, 0)

    def collect(d, acc):
        tile_copy(d).wait_recv()
        return acc + got[d].astype(f32)

    acc = lax.fori_loop(1, n, collect, product(me))
    inter_ref[...] = acc[:, :columns]
    ham_ref[...] = acc[:, columns:]

    for copy in started:
        copy.wait_send()

    def drain(d, carry):
        tile_copy(d).wait_send()
        return carry

    lax.fori_loop(1, n, drain, 0)


def on_device(n, nb, band_block, band_basis, mass_scale, cell_matrices, cell_nodes, cell_count, send_index):
    columns, owned = band_block.shape
    cell_slots, corners = cell_nodes.shape
    width, slots = send_index.shape[1:]
    cols = band_basis.shape[1]
    bands = cols * nb
    rows = bands // n
    count = cell_slots * corners
    total = owned + width * slots
    live = jnp.arange(cell_slots, dtype=jnp.int32)[:, None] < cell_count[0]
    nodes = jnp.where(live, cell_nodes, -1)
    vmem = pl.BlockSpec(memory_space=pltpu.VMEM)
    return pl.pallas_call(
        functools.partial(kernel, n, nb, width),
        out_shape=(
            jax.ShapeDtypeStruct((columns, owned), bf16),
            jax.ShapeDtypeStruct((rows, columns), f32),
            jax.ShapeDtypeStruct((rows, columns), f32),
        ),
        in_specs=[vmem, pl.BlockSpec(memory_space=pl.ANY)] + [vmem] * 6,
        out_specs=(vmem, vmem, vmem),
        scratch_shapes=[
            pltpu.VMEM((bands, owned), bf16),
            pltpu.VMEM((total, total), bf16),
            pltpu.VMEM((count, total), bf16),
            pltpu.VMEM((owned, 2 * columns), bf16),
            pltpu.VMEM((4, width * slots, columns), bf16),
            pltpu.VMEM((4, width * slots, columns), bf16),
            pltpu.VMEM((4, width * slots, columns), bf16),
            pltpu.VMEM((4, width * slots, columns), bf16),
            pltpu.VMEM((n, rows, 2 * columns), bf16),
            pltpu.VMEM((n, rows, 2 * columns), bf16),
            pltpu.SemaphoreType.DMA((8, width)),
            pltpu.SemaphoreType.DMA((8, width)),
            pltpu.SemaphoreType.DMA((nb,)),
            pltpu.SemaphoreType.DMA((nb,)),
            pltpu.SemaphoreType.DMA,
            pltpu.SemaphoreType.DMA((n,)),
            pltpu.SemaphoreType.DMA((n,)),
        ],
        compiler_params=pltpu.CompilerParams(collective_id=0, has_side_effects=True),
    )(
        band_block,
        band_basis.T,
        mass_scale.reshape(owned, 1),
        cell_matrices.reshape(count, corners),
        nodes.reshape(count, 1),
        nodes.reshape(1, count),
        send_index.reshape(width * slots, 1),
        send_index.reshape(1, width * slots),
    )


def solution(mesh):
    placed = (
        P("band", "mesh"),
        P("mesh", "band"),
        P("mesh"),
        P("mesh", None),
        P("mesh", None),
        P("mesh"),
        P("mesh", None, None),
    )
    return jax.shard_map(
        functools.partial(on_device, mesh.shape["mesh"], mesh.shape["band"]),
        mesh=mesh,
        in_specs=placed,
        out_specs=(P("band", "mesh"), P("mesh", "band"), P("mesh", "band")),
        check_vma=False,
    )
```

```python
import functools
import math
import jax
import jax.numpy as jnp
from jax import lax
from jax.experimental import pallas as pl
from jax.experimental.pallas import tpu as pltpu
from jax.sharding import PartitionSpec as P

filter_centre = 1.5
filter_half = 2.5
first_sigma = -0.625
MESH = pl.DeviceIdType.MESH
bf16 = jnp.bfloat16
f32 = jnp.float32


def sigma_values():
    values = [first_sigma]
    for _ in range(2):
        values.append(1.0 / (2.0 / first_sigma - values[-1]))
    return values


def neighbour_offset(neighbour, reach):
    if neighbour < reach:
        return neighbour + 1
    return reach - 1 - neighbour


def dot(a, b):
    return jnp.dot(a, b, preferred_element_type=f32)


def dot_nt(a, b):
    return lax.dot_general(a, b, (((1,), (1,)), ((), ())), preferred_element_type=f32)


def kernel(
    n, nb, group, packed, x_ref, basis_ref, mass_ref, mats_ref, nodes_ref, count_ref, send_ref,
    f_ref, inter_ref, ham_ref,
    full, hots, coupled, out_x, ghost, out_y, back, held, tile, got,
    halo_send, halo_recv, basis_send, basis_recv, held_send, held_recv, tile_send, tile_recv,
):
    me = lax.axis_index("mesh")
    mine = lax.axis_index("band")
    seat = lax.rem(me, group)
    team = me // group
    teams = n // group
    columns, owned = x_ref.shape
    width, slots = send_ref.shape[1:]
    reach = width // 2
    rows = full.shape[2]
    per_band = n // nb
    per_seat = per_band // group
    total = owned + width * slots
    cells, corners = nodes_ref.shape

    barrier = pltpu.get_barrier_semaphore()

    def greet(d, carry):
        pl.semaphore_signal(
            barrier, inc=1, device_id=(lax.rem(me + d, n), mine), device_id_type=MESH
        )
        return carry

    lax.fori_loop(1, n, greet, 0)
    for d in range(1, nb):
        for e in range(group):
            pl.semaphore_signal(
                barrier,
                inc=1,
                device_id=(team * group + lax.rem(seat + e, group), lax.rem(mine + d, nb)),
                device_id_type=MESH,
            )

    def basis_copy(e, d, s):
        chunk = lax.rem(seat + e, group) + group * s
        source = basis_ref.at[pl.ds(pl.multiple_of(chunk * rows, 16), rows)]
        target = full.at[seat, mine * per_seat + s]
        if e == 0 and d == 0:
            return pltpu.make_async_copy(source, target, basis_recv.at[e, d, s])
        return pltpu.make_async_remote_copy(
            src_ref=source,
            dst_ref=target,
            send_sem=basis_send.at[e, d, s],
            recv_sem=basis_recv.at[e, d, s],
            device_id=(team * group + lax.rem(seat + e, group), lax.rem(mine + d, nb)),
            device_id_type=MESH,
        )

    def basis_wait(e, d, s):
        if e == 0 and d == 0:
            basis_copy(e, d, s).wait()
            return
        copy = pltpu.make_async_remote_copy(
            src_ref=basis_ref.at[pl.ds(0, rows)],
            dst_ref=full.at[lax.rem(seat + group - e, group), lax.rem(mine + nb - d, nb) * per_seat + s],
            send_sem=basis_send.at[e, d, s],
            recv_sem=basis_recv.at[e, d, s],
            device_id=(team * group + lax.rem(seat + e, group), lax.rem(mine + d, nb)),
            device_id_type=MESH,
        )
        copy.wait_recv()

    places = [(e, d, s) for s in range(per_seat) for d in range(nb) for e in range(group)]
    away = [place for place in places if place[:2] != (0, 0)]
    for s in range(per_seat):
        basis_copy(0, 0, s).start()

    mass = jnp.broadcast_to(mass_ref[...], (8, owned)).T[:, :1]
    owned_ids = lax.broadcasted_iota(jnp.int32, (owned, slots), 0)
    hot_parts = [
        jnp.where(owned_ids == send_ref[0, k : k + 1, :], 1.0, 0.0) for k in range(width)
    ]
    send_hot_f = jnp.concatenate(hot_parts, axis=1)
    send_hot_t = send_hot_f.astype(bf16)
    send_hot = send_hot_f.T.astype(bf16)
    live = count_ref[0]
    total_ids = lax.broadcasted_iota(jnp.int32, (total, corners), 0)
    for c in range(cells):
        hot = jnp.where(
            jnp.logical_and(total_ids == nodes_ref[c : c + 1, :], c < live), 1.0, 0.0
        ).astype(bf16)
        part = slice(c * corners, (c + 1) * corners)
        hots[:, part] = hot
        coupled[:, part] = dot_nt(hot, mats_ref[part, :]).astype(bf16)

    previous = x_ref[...].astype(f32).T.astype(bf16)

    pl.semaphore_wait(barrier, n - 1 + (nb - 1) * group)

    def halo(source, target, index):
        copies = []
        for k in range(width):
            partner = (k + reach) % width
            to = lax.rem(me + neighbour_offset(k, reach) + n, n)
            copies.append(
                pltpu.make_async_remote_copy(
                    src_ref=source.at[pl.ds(k * slots, slots)],
                    dst_ref=target.at[pl.ds(partner * slots, slots)],
                    send_sem=halo_send.at[index, k],
                    recv_sem=halo_recv.at[index, partner],
                    device_id=(to, mine),
                    device_id_type=MESH,
                )
            )
        return copies

    started = []
    stiff = []
    share = -(-len(away) // 5)

    def held_copy(which, e):
        return pltpu.make_async_remote_copy(
            src_ref=held.at[which, seat],
            dst_ref=held.at[which, seat],
            send_sem=held_send.at[which, e],
            recv_sem=held_recv.at[which, e],
            device_id=(team * group + lax.rem(seat + e, group), mine),
            device_id_type=MESH,
        )

    def held_wait(which, e):
        there = lax.rem(seat + group - e, group)
        copy = pltpu.make_async_remote_copy(
            src_ref=held.at[which, seat],
            dst_ref=held.at[which, there],
            send_sem=held_send.at[which, e],
            recv_sem=held_recv.at[which, e],
            device_id=(team * group + lax.rem(seat + e, group), mine),
            device_id_type=MESH,
        )
        copy.wait_recv()

    def share_field(which):
        for e in range(1, group):
            held_copy(which, e).start()

    def product(which, place):
        value = dot_nt(held[which, 0], full[0, place])
        for i in range(1, group):
            value = value + dot_nt(held[which, i], full[i, place])
        return value

    def pack(value):
        if not packed:
            return value
        half = columns // 2
        left = rows - rows % 128
        rest = jnp.concatenate([value[:half, left:], value[half:, left:]], axis=1)
        parts = [value[:, a : a + 128] for a in range(0, left, 128)]
        return jnp.concatenate(parts + [rest], axis=0)

    def unpack(value):
        if not packed:
            return value
        half = columns // 2
        full_parts = rows // 128
        parts = [value[a * columns : (a + 1) * columns] for a in range(full_parts)]
        rest = value[full_parts * columns :]
        parts.append(jnp.concatenate([rest[:, :64], rest[:, 64:]], axis=0))
        return jnp.concatenate(parts, axis=1)

    def tile_copy(which, d):
        return pltpu.make_async_remote_copy(
            src_ref=tile.at[which, d],
            dst_ref=got.at[which, d],
            send_sem=tile_send.at[which, d],
            recv_sem=tile_recv.at[which, d],
            device_id=(lax.rem(team + d, teams) * group + seat, mine),
            device_id_type=MESH,
        )

    def tiles_out(which):
        for e in range(1, group):
            held_wait(which, e)

        def emit(d, carry):
            tile[which, d] = pack(product(which, lax.rem(team + d, teams))).astype(bf16)
            tile_copy(which, d).start()
            return carry

        lax.fori_loop(1, teams, emit, 0)

    def tiles_in(which):
        def collect(d, acc):
            tile_copy(which, d).wait_recv()
            return acc + got[which, d].astype(f32)

        return unpack(lax.fori_loop(1, teams, collect, pack(product(which, team))))

    def after_send(index):
        for place in away[share * index : share * (index + 1)]:
            basis_copy(*place).start()
        if index == 6:
            share_field(0)
        if index == 7:
            for place in places:
                basis_wait(*place)
            tiles_out(0)

    def operate(step, field):
        scaled = (mass * field.astype(f32)).astype(bf16)
        out_x[step] = dot(send_hot, scaled).astype(bf16)
        copies = halo(out_x.at[step], ghost.at[step], 2 * step)
        for copy in copies:
            copy.start()
        started.extend(copies)
        after_send(2 * step)
        if step == 0:
            stiff.append(dot_nt(hots[...], coupled[...]).astype(bf16))
        matrix = stiff[0]
        edge = dot(matrix[owned:, :owned], scaled)
        inner = dot(matrix[:owned, :owned], scaled)
        for copy in copies:
            copy.wait_recv()
        ghosts = ghost[step]
        out_y[step] = (edge + dot(matrix[owned:, owned:], ghosts)).astype(bf16)
        copies = halo(out_y.at[step], back.at[step], 2 * step + 1)
        for copy in copies:
            copy.start()
        started.extend(copies)
        after_send(2 * step + 1)
        inner = inner + dot(matrix[:owned, owned:], ghosts)
        for copy in copies:
            copy.wait_recv()
        return mass * (inner + dot(send_hot_t, back[step]))

    sigmas = sigma_values()
    applied = operate(0, previous)
    current = (
        (applied - filter_centre * previous.astype(f32)) * (sigmas[0] / filter_half)
    ).astype(bf16)
    for step in range(1, 3):
        applied = operate(step, current)
        scale_now = 2.0 * sigmas[step] / filter_half
        mixing = sigmas[step - 1] * sigmas[step]
        update = (applied - filter_centre * current.astype(f32)) * scale_now - mixing * previous.astype(f32)
        previous = current
        current = update.astype(bf16)
    turned = current.astype(f32).T.astype(bf16)
    f_ref[...] = turned
    held[0, seat] = turned
    image = operate(3, current)
    held[1, seat] = image.T.astype(bf16)
    share_field(1)
    inter_own = tiles_in(0)
    tiles_out(1)
    inter_ref[...] = inter_own
    ham_ref[...] = tiles_in(1)

    for copy in started:
        copy.wait_send()
    for place in away:
        basis_copy(*place).wait_send()
    for which in range(2):
        for e in range(1, group):
            held_copy(which, e).wait_send()

        def drain(d, carry):
            tile_copy(which, d).wait_send()
            return carry

        lax.fori_loop(1, teams, drain, 0)


def on_device(n, nb, band_block, band_basis, mass_scale, cell_matrices, cell_nodes, cell_count, send_index):
    columns, owned = band_block.shape
    cell_slots, corners = cell_nodes.shape
    width, slots = send_index.shape[1:]
    cols = band_basis.shape[1]
    rows = cols * nb // n
    count = cell_slots * corners
    total = owned + width * slots
    group = math.gcd(4, n // nb)
    teams = n // group
    packed = rows % 128 == 64 and columns % 32 == 0
    tile_shape = (columns * rows // 128, 128) if packed else (columns, rows)
    vmem = pl.BlockSpec(memory_space=pltpu.VMEM)
    smem = pl.BlockSpec(memory_space=pltpu.SMEM)
    edge_shape = pltpu.VMEM((4, width * slots, columns), bf16)
    filtered, inter, ham = pl.pallas_call(
        functools.partial(kernel, n, nb, group, packed),
        out_shape=(
            jax.ShapeDtypeStruct((columns, owned), bf16),
            jax.ShapeDtypeStruct((columns, rows), f32),
            jax.ShapeDtypeStruct((columns, rows), f32),
        ),
        in_specs=[vmem, pl.BlockSpec(memory_space=pl.ANY), vmem, vmem, vmem, smem, vmem],
        out_specs=(vmem, vmem, vmem),
        scratch_shapes=[
            pltpu.VMEM((group, teams, rows, owned), bf16),
            pltpu.VMEM((total, count), bf16),
            pltpu.VMEM((total, count), bf16),
            edge_shape,
            edge_shape,
            edge_shape,
            edge_shape,
            pltpu.VMEM((2, group, columns, owned), bf16),
            pltpu.VMEM((2, teams) + tile_shape, bf16),
            pltpu.VMEM((2, teams) + tile_shape, bf16),
            pltpu.SemaphoreType.DMA((8, width)),
            pltpu.SemaphoreType.DMA((8, width)),
            pltpu.SemaphoreType.DMA((group, nb, n // nb // group)),
            pltpu.SemaphoreType.DMA((group, nb, n // nb // group)),
            pltpu.SemaphoreType.DMA((2, group)),
            pltpu.SemaphoreType.DMA((2, group)),
            pltpu.SemaphoreType.DMA((2, teams)),
            pltpu.SemaphoreType.DMA((2, teams)),
        ],
        compiler_params=pltpu.CompilerParams(collective_id=0, has_side_effects=True),
    )(
        band_block,
        band_basis.T,
        mass_scale.reshape(1, owned),
        cell_matrices.reshape(count, corners),
        cell_nodes,
        cell_count,
        send_index,
    )
    return filtered, inter.T, ham.T


def solution(mesh):
    placed = (
        P("band", "mesh"),
        P("mesh", "band"),
        P("mesh"),
        P("mesh", None),
        P("mesh", None),
        P("mesh"),
        P("mesh", None, None),
    )
    return jax.shard_map(
        functools.partial(on_device, mesh.shape["mesh"], mesh.shape["band"]),
        mesh=mesh,
        in_specs=placed,
        out_specs=(P("band", "mesh"), P("mesh", "band"), P("mesh", "band")),
        check_vma=False,
    )
```

```python
import functools
import math
import jax
import jax.numpy as jnp
from jax import lax
from jax.experimental import pallas as pl
from jax.experimental.pallas import tpu as pltpu
from jax.sharding import PartitionSpec as P

filter_centre = 1.5
filter_half = 2.5
first_sigma = -0.625
MESH = pl.DeviceIdType.MESH
bf16 = jnp.bfloat16
f32 = jnp.float32


def sigma_values():
    values = [first_sigma]
    for _ in range(2):
        values.append(1.0 / (2.0 / first_sigma - values[-1]))
    return values


def neighbour_offset(neighbour, reach):
    if neighbour < reach:
        return neighbour + 1
    return reach - 1 - neighbour


def dot(a, b):
    return jnp.dot(a, b, preferred_element_type=f32)


def dot_nt(a, b):
    return lax.dot_general(a, b, (((1,), (1,)), ((), ())), preferred_element_type=f32)


def kernel(
    n, nb, group, packed, x_ref, basis_ref, mass_ref, mats_ref, nodes_ref, count_ref, send_ref,
    f_ref, inter_ref, ham_ref,
    full, block, turned_basis, hots, coupled, out_x, ghost, out_y, back, held, tile, got,
    halo_send, halo_recv, block_sem, basis_send, basis_recv, held_send, held_recv, tile_send, tile_recv,
):
    me = lax.axis_index("mesh")
    mine = lax.axis_index("band")
    seat = lax.rem(me, group)
    team = me // group
    teams = n // group
    columns, owned = x_ref.shape
    width, slots = send_ref.shape[1:]
    reach = width // 2
    rows = full.shape[2]
    per_band = n // nb
    per_seat = per_band // group
    total = owned + width * slots
    cells, corners = nodes_ref.shape

    barrier = pltpu.get_barrier_semaphore()

    def greet(d, carry):
        pl.semaphore_signal(
            barrier, inc=1, device_id=(lax.rem(me + d, n), mine), device_id_type=MESH
        )
        return carry

    lax.fori_loop(1, n, greet, 0)
    for d in range(1, nb):
        for e in range(group):
            pl.semaphore_signal(
                barrier,
                inc=1,
                device_id=(team * group + lax.rem(seat + e, group), lax.rem(mine + d, nb)),
                device_id_type=MESH,
            )

    def basis_copy(e, d, s):
        chunk = lax.rem(seat + e, group) + group * s
        source = turned_basis.at[pl.ds(pl.multiple_of(chunk * rows, 16), rows)]
        target = full.at[seat, mine * per_seat + s]
        if e == 0 and d == 0:
            return pltpu.make_async_copy(source, target, basis_recv.at[e, d, s])
        return pltpu.make_async_remote_copy(
            src_ref=source,
            dst_ref=target,
            send_sem=basis_send.at[e, d, s],
            recv_sem=basis_recv.at[e, d, s],
            device_id=(team * group + lax.rem(seat + e, group), lax.rem(mine + d, nb)),
            device_id_type=MESH,
        )

    def basis_wait(e, d, s):
        if e == 0 and d == 0:
            basis_copy(e, d, s).wait()
            return
        copy = pltpu.make_async_remote_copy(
            src_ref=turned_basis.at[pl.ds(0, rows)],
            dst_ref=full.at[lax.rem(seat + group - e, group), lax.rem(mine + nb - d, nb) * per_seat + s],
            send_sem=basis_send.at[e, d, s],
            recv_sem=basis_recv.at[e, d, s],
            device_id=(team * group + lax.rem(seat + e, group), lax.rem(mine + d, nb)),
            device_id_type=MESH,
        )
        copy.wait_recv()

    places = [(e, d, s) for s in range(per_seat) for d in range(nb) for e in range(group)]
    away = [place for place in places if place[:2] != (0, 0)]
    load = pltpu.make_async_copy(basis_ref, block, block_sem)
    load.start()

    mass = jnp.broadcast_to(mass_ref[...], (8, owned)).T[:, :1]
    owned_ids = lax.broadcasted_iota(jnp.int32, (owned, slots), 0)
    hot_parts = [
        jnp.where(owned_ids == send_ref[0, k : k + 1, :], 1.0, 0.0) for k in range(width)
    ]
    send_hot_f = jnp.concatenate(hot_parts, axis=1)
    send_hot_t = send_hot_f.astype(bf16)
    send_hot = send_hot_f.T.astype(bf16)
    live = count_ref[0]
    total_ids = lax.broadcasted_iota(jnp.int32, (total, corners), 0)
    for c in range(cells):
        hot = jnp.where(
            jnp.logical_and(total_ids == nodes_ref[c : c + 1, :], c < live), 1.0, 0.0
        ).astype(bf16)
        part = slice(c * corners, (c + 1) * corners)
        hots[:, part] = hot
        coupled[:, part] = dot_nt(hot, mats_ref[part, :]).astype(bf16)

    previous = x_ref[...].astype(f32).T.astype(bf16)

    load.wait()
    for a in range(0, block.shape[1], 128):
        turned_basis[a : a + 128, :] = block[:, a : a + 128].T
    for s in range(per_seat):
        basis_copy(0, 0, s).start()

    pl.semaphore_wait(barrier, n - 1 + (nb - 1) * group)

    def halo(source, target, index):
        copies = []
        for k in range(width):
            partner = (k + reach) % width
            to = lax.rem(me + neighbour_offset(k, reach) + n, n)
            copies.append(
                pltpu.make_async_remote_copy(
                    src_ref=source.at[pl.ds(k * slots, slots)],
                    dst_ref=target.at[pl.ds(partner * slots, slots)],
                    send_sem=halo_send.at[index, k],
                    recv_sem=halo_recv.at[index, partner],
                    device_id=(to, mine),
                    device_id_type=MESH,
                )
            )
        return copies

    started = []
    stiff = []
    share = -(-len(away) // 5)

    def held_copy(which, e):
        return pltpu.make_async_remote_copy(
            src_ref=held.at[which, seat],
            dst_ref=held.at[which, seat],
            send_sem=held_send.at[which, e],
            recv_sem=held_recv.at[which, e],
            device_id=(team * group + lax.rem(seat + e, group), mine),
            device_id_type=MESH,
        )

    def held_wait(which, e):
        there = lax.rem(seat + group - e, group)
        copy = pltpu.make_async_remote_copy(
            src_ref=held.at[which, seat],
            dst_ref=held.at[which, there],
            send_sem=held_send.at[which, e],
            recv_sem=held_recv.at[which, e],
            device_id=(team * group + lax.rem(seat + e, group), mine),
            device_id_type=MESH,
        )
        copy.wait_recv()

    def share_field(which):
        for e in range(1, group):
            held_copy(which, e).start()

    def product(which, place):
        value = dot_nt(held[which, 0], full[0, place])
        for i in range(1, group):
            value = value + dot_nt(held[which, i], full[i, place])
        return value

    def pack(value):
        if not packed:
            return value
        half = columns // 2
        left = rows - rows % 128
        rest = jnp.concatenate([value[:half, left:], value[half:, left:]], axis=1)
        parts = [value[:, a : a + 128] for a in range(0, left, 128)]
        return jnp.concatenate(parts + [rest], axis=0)

    def unpack(value):
        if not packed:
            return value
        half = columns // 2
        full_parts = rows // 128
        parts = [value[a * columns : (a + 1) * columns] for a in range(full_parts)]
        rest = value[full_parts * columns :]
        parts.append(jnp.concatenate([rest[:, :64], rest[:, 64:]], axis=0))
        return jnp.concatenate(parts, axis=1)

    def tile_copy(which, d):
        return pltpu.make_async_remote_copy(
            src_ref=tile.at[which, d],
            dst_ref=got.at[which, d],
            send_sem=tile_send.at[which, d],
            recv_sem=tile_recv.at[which, d],
            device_id=(lax.rem(team + d, teams) * group + seat, mine),
            device_id_type=MESH,
        )

    def tiles_out(which):
        for e in range(1, group):
            held_wait(which, e)

        def emit(d, carry):
            tile[which, d] = pack(product(which, lax.rem(team + d, teams))).astype(bf16)
            tile_copy(which, d).start()
            return carry

        lax.fori_loop(1, teams, emit, 0, unroll=teams <= 4)

    def tiles_in(which, own):
        def collect(d, acc):
            tile_copy(which, d).wait_recv()
            return acc + got[which, d].astype(f32)

        return unpack(lax.fori_loop(1, teams, collect, own, unroll=teams <= 4))

    def after_send(index):
        for place in away[share * index : share * (index + 1)]:
            basis_copy(*place).start()
        if index == 6:
            share_field(0)
        if index == 7:
            for place in places:
                basis_wait(*place)

    def operate(step, field):
        scaled = (mass * field.astype(f32)).astype(bf16)
        out_x[step] = dot(send_hot, scaled).astype(bf16)
        copies = halo(out_x.at[step], ghost.at[step], 2 * step)
        for copy in copies:
            copy.start()
        started.extend(copies)
        after_send(2 * step)
        if step == 0:
            stiff.append(dot_nt(hots[...], coupled[...]).astype(bf16))
        matrix = stiff[0]
        edge = dot(matrix[owned:, :owned], scaled)
        inner = dot(matrix[:owned, :owned], scaled)
        for copy in copies:
            copy.wait_recv()
        ghosts = ghost[step]
        out_y[step] = (edge + dot(matrix[owned:, owned:], ghosts)).astype(bf16)
        copies = halo(out_y.at[step], back.at[step], 2 * step + 1)
        for copy in copies:
            copy.start()
        started.extend(copies)
        after_send(2 * step + 1)
        inner = inner + dot(matrix[:owned, owned:], ghosts)
        for copy in copies:
            copy.wait_recv()
        return mass * (inner + dot(send_hot_t, back[step]))

    sigmas = sigma_values()
    applied = operate(0, previous)
    current = (
        (applied - filter_centre * previous.astype(f32)) * (sigmas[0] / filter_half)
    ).astype(bf16)
    for step in range(1, 3):
        applied = operate(step, current)
        scale_now = 2.0 * sigmas[step] / filter_half
        mixing = sigmas[step - 1] * sigmas[step]
        update = (applied - filter_centre * current.astype(f32)) * scale_now - mixing * previous.astype(f32)
        previous = current
        current = update.astype(bf16)
    turned = current.astype(f32).T.astype(bf16)
    f_ref[...] = turned
    held[0, seat] = turned
    image = operate(3, current)
    held[1, seat] = image.T.astype(bf16)
    share_field(1)
    tiles_out(0)
    inter_own = pack(product(0, team))
    tiles_out(1)
    ham_own = pack(product(1, team))
    inter_ref[...] = tiles_in(0, inter_own)
    ham_ref[...] = tiles_in(1, ham_own)

    for copy in started:
        copy.wait_send()
    for place in away:
        basis_copy(*place).wait_send()
    for which in range(2):
        for e in range(1, group):
            held_copy(which, e).wait_send()

        def drain(d, carry):
            tile_copy(which, d).wait_send()
            return carry

        lax.fori_loop(1, teams, drain, 0)


def on_device(n, nb, band_block, band_basis, mass_scale, cell_matrices, cell_nodes, cell_count, send_index):
    columns, owned = band_block.shape
    cell_slots, corners = cell_nodes.shape
    width, slots = send_index.shape[1:]
    cols = band_basis.shape[1]
    rows = cols * nb // n
    count = cell_slots * corners
    total = owned + width * slots
    group = math.gcd(4, n // nb)
    teams = n // group
    packed = rows % 128 == 64 and columns % 32 == 0
    tile_shape = (columns * rows // 128, 128) if packed else (columns, rows)
    vmem = pl.BlockSpec(memory_space=pltpu.VMEM)
    smem = pl.BlockSpec(memory_space=pltpu.SMEM)
    edge_shape = pltpu.VMEM((4, width * slots, columns), bf16)
    filtered, inter, ham = pl.pallas_call(
        functools.partial(kernel, n, nb, group, packed),
        out_shape=(
            jax.ShapeDtypeStruct((columns, owned), bf16),
            jax.ShapeDtypeStruct((columns, rows), f32),
            jax.ShapeDtypeStruct((columns, rows), f32),
        ),
        in_specs=[vmem, pl.BlockSpec(memory_space=pl.ANY), vmem, vmem, vmem, smem, vmem],
        out_specs=(vmem, vmem, vmem),
        scratch_shapes=[
            pltpu.VMEM((group, teams, rows, owned), bf16),
            pltpu.VMEM((owned, cols), bf16),
            pltpu.VMEM((cols, owned), bf16),
            pltpu.VMEM((total, count), bf16),
            pltpu.VMEM((total, count), bf16),
            edge_shape,
            edge_shape,
            edge_shape,
            edge_shape,
            pltpu.VMEM((2, group, columns, owned), bf16),
            pltpu.VMEM((2, teams) + tile_shape, bf16),
            pltpu.VMEM((2, teams) + tile_shape, bf16),
            pltpu.SemaphoreType.DMA((8, width)),
            pltpu.SemaphoreType.DMA((8, width)),
            pltpu.SemaphoreType.DMA,
            pltpu.SemaphoreType.DMA((group, nb, n // nb // group)),
            pltpu.SemaphoreType.DMA((group, nb, n // nb // group)),
            pltpu.SemaphoreType.DMA((2, group)),
            pltpu.SemaphoreType.DMA((2, group)),
            pltpu.SemaphoreType.DMA((2, teams)),
            pltpu.SemaphoreType.DMA((2, teams)),
        ],
        compiler_params=pltpu.CompilerParams(collective_id=0, has_side_effects=True),
    )(
        band_block,
        band_basis,
        mass_scale.reshape(1, owned),
        cell_matrices.reshape(count, corners),
        cell_nodes,
        cell_count,
        send_index,
    )
    return filtered, inter.T, ham.T


def solution(mesh):
    placed = (
        P("band", "mesh"),
        P("mesh", "band"),
        P("mesh"),
        P("mesh", None),
        P("mesh", None),
        P("mesh"),
        P("mesh", None, None),
    )
    return jax.shard_map(
        functools.partial(on_device, mesh.shape["mesh"], mesh.shape["band"]),
        mesh=mesh,
        in_specs=placed,
        out_specs=(P("band", "mesh"), P("mesh", "band"), P("mesh", "band")),
        check_vma=False,
    )
```
